32 devices in a mesh: leaf: 8 (over y, x, core), probe: 4 (over z).
Axes of the slice: x: 2, y: 2, z: 4, core: 2. Of those that a mesh axis runs over, the one named last changes fastest.
Arguments:
- leaf_blocks: float32 [8192, 1024], P('leaf'), may hold values from -0.1875 to 0.1875
- block_mask: int32 [8, 8, 8], P('leaf'), may hold values 0 or 1
- row_factor_stack: float32 [3, 8192, 128], P(None, 'leaf'), may hold values from -0.5 to 0.5
- column_factor_stack: float32 [3, 8192, 128], P(None, 'leaf'), may hold values from -0.0625 to 0.0625
- probes: float32 [8192, 1024], P('leaf', 'probe'), may hold values from -6 to 6
Outputs:
- applied: float32 [8192, 1024], P('leaf', 'probe')
- probe_gram: float32 [1024, 1024], P('leaf', 'probe')
The draws below stay inside these ranges and needn't reach their ends.
All inputs are finite; a program needn't handle non-finite values. No bound on the sum of `block_mask` on one device may be relied on, other than what follows from the above.
Results may differ from the reference program's by a relative error of at most 0.0001.
Values sent between devices are 32-bit elements; how exact they have to be, the bound alone decides.
A program may use at most 64 MiB of HBM per device.

```python
import jax
import jax.numpy as jnp
from jax import lax

LEAF_PTS = 1024
MB = 8
RANK = 128
PROBES = 1024
LEVELS = 3
POINTS = 8192
N_LEAF = 8


def touch_ends(drawn, key, smallest, high):
    longest = drawn.shape.index(max(drawn.shape))
    spots = []
    for shift in (0, 1):
        where = [jax.random.randint(jax.random.fold_in(key, axis), (), 0, length) for axis, length in enumerate(drawn.shape)]
        where[longest] = (where[longest] + shift) % drawn.shape[longest]
        spots.append(tuple(where))
    return drawn.at[spots[0]].set(smallest).at[spots[1]].set(high)


def block_scale(key, dims, shards, least, largest):
    loudness, own = 1.0, jax.random.fold_in(key, 6)
    for dim, blocks in shards:
        steps = jnp.exp(jax.random.uniform(jax.random.fold_in(own, dim), (blocks,), jnp.float32, least / len(shards), largest / len(shards)))
        loudness = loudness * jnp.repeat(steps, dims[dim] // blocks).reshape([-1 if axis == dim else 1 for axis in range(len(dims))])
    return loudness


def normal_values(key, dims, deviation, bound, cuts=(), kind=jnp.bfloat16):
    values = jax.random.normal(key, dims, jnp.float32) * deviation
    if len(cuts) > 0:
        values = block_scale(key, dims, cuts, -0.22, 0.18) * values
    return jnp.clip(values, min=-bound, max=bound).astype(kind)


def setup_inputs(seed: int = 0) -> dict:
    keys = jax.random.split(jax.random.key(seed), 6)
    leaf_blocks = normal_values(keys[0], (POINTS, LEAF_PTS), LEAF_PTS ** -0.5, 0.1875, ((0, 8),), jnp.float32)
    block_mask = touch_ends((jax.random.randint(keys[1], (N_LEAF, MB, MB), 0, 4) < 3).astype(jnp.int32), jax.random.fold_in(keys[1], 1), 0, 1)
    row_factor_stack = normal_values(keys[2], (LEVELS, POINTS, RANK), RANK ** -0.5, 0.5, ((1, 8),), jnp.float32)
    column_factor_stack = normal_values(keys[3], (LEVELS, POINTS, RANK), POINTS ** -0.5, 0.0625, ((1, 8),), jnp.float32)
    probes = normal_values(keys[4], (POINTS, PROBES), 1.0, 6.0, ((0, 8), (1, 4)), jnp.float32)
    return {"leaf_blocks": leaf_blocks, "block_mask": block_mask, "row_factor_stack": row_factor_stack, "column_factor_stack": column_factor_stack, "probes": probes}


def leaf_product(inputs):
    block, weights, columns = inputs
    block_span_width = LEAF_PTS // MB
    spread = jnp.repeat(jnp.repeat(weights.astype(jnp.float32), block_span_width, 0), block_span_width, 1)
    return jnp.dot(block * spread, columns, precision=lax.Precision.HIGHEST, preferred_element_type=jnp.float32)


def reference(leaf_blocks, block_mask, row_factor_stack, column_factor_stack, probes):
    block_list = leaf_blocks.reshape(N_LEAF, LEAF_PTS, LEAF_PTS)
    columns = probes.reshape(N_LEAF, LEAF_PTS, PROBES)
    applied = lax.map(leaf_product, (block_list, block_mask, columns)).reshape(POINTS, PROBES)
    for level in range(LEVELS):
        width = LEAF_PTS * 2 ** level
        cluster_groups = POINTS // width
        grouped = probes.reshape(cluster_groups, width, PROBES)
        right_part = column_factor_stack[level].reshape(cluster_groups, width, RANK)
        probe_projected = jnp.einsum("bsr,bsp->brp", right_part, grouped, precision=lax.Precision.HIGHEST)
        swapped = probe_projected.reshape(cluster_groups // 2, 2, RANK, PROBES)[:, ::-1].reshape(cluster_groups, RANK, PROBES)
        left_part = row_factor_stack[level].reshape(cluster_groups, width, RANK)
        applied = applied + jnp.einsum("bsr,brp->bsp", left_part, swapped, precision=lax.Precision.HIGHEST).reshape(POINTS, PROBES)
    probe_gram = jnp.dot(applied.T, applied, precision=lax.Precision.HIGHEST, preferred_element_type=jnp.float32) / POINTS
    return applied, probe_gram
```

```python
import functools

import jax
import jax.numpy as jnp
from jax import lax
from jax.experimental import pallas as pl
from jax.experimental.pallas import tpu as pltpu
from jax.sharding import PartitionSpec as P

MESH = pl.DeviceIdType.MESH
CONTRACT_ROWS = (((0,), (0,)), ((), ()))
PLAIN = (((1,), (0,)), ((), ()))


def split(value):
    high = value.astype(jnp.bfloat16)
    return high, (value - high.astype(jnp.float32)).astype(jnp.bfloat16)


def dot3(left, right, dims):
    (lh, ll), (rh, rl) = left, right
    dot = functools.partial(lax.dot_general, dimension_numbers=dims, preferred_element_type=jnp.float32)
    return dot(lh, rh) + (dot(lh, rl) + dot(ll, rh))


def kernel(
    n_leaf, n_probe, pieces,
    mask, block_hbm, row_hbm, col_hbm, probe_hbm, app_hbm, gram_ref,
    block, row, col, probe, probe_h, probe_l, own, swap, sib_h, sib_l,
    app, app_h, app_l, got, part, shares, total, extra, turned,
    load_sem, out_sem, swap_send, swap_recv, right_send, right_recv, left_send, left_recv,
    share_send, share_recv, extra_send, extra_recv,
):
    depth, rank = row.shape[0], row.shape[2]
    points, width = app.shape
    side = mask.shape[1]
    span = points // side
    half = points // 2
    piece = half // pieces
    leaf, z = lax.axis_index("leaf"), lax.axis_index("probe")
    slab = n_probe * width // n_leaf
    fan = n_leaf // n_probe
    a, b = leaf // fan, leaf % fan
    last = n_probe - 1
    ends = n_probe > 2

    loads = [
        pltpu.make_async_copy(source, target, load_sem.at[i])
        for i, (source, target) in enumerate(
            ((probe_hbm, probe), (col_hbm, col), (block_hbm, block), (row_hbm, row))
        )
    ]
    for load in loads:
        load.start()

    barrier = pltpu.get_barrier_semaphore()

    @pl.loop(1, n_leaf)
    def _(k):
        pl.semaphore_signal(
            barrier, inc=1, device_id={"leaf": (leaf + k) % n_leaf, "probe": z}, device_id_type=MESH
        )

    @pl.when(z > 0)
    def _():
        pl.semaphore_signal(barrier, inc=1, device_id={"leaf": leaf, "probe": z - 1}, device_id_type=MESH)

    @pl.when(z < last)
    def _():
        pl.semaphore_signal(barrier, inc=1, device_id={"leaf": leaf, "probe": z + 1}, device_id_type=MESH)

    @pl.when(a != z)
    def _():
        @pl.loop(0, fan)
        def _(c):
            pl.semaphore_signal(
                barrier, inc=1, device_id={"leaf": z * fan + c, "probe": a}, device_id_type=MESH
            )

    loads[0].wait()
    ph, plo = split(probe[...])
    probe_h[...] = ph
    probe_l[...] = plo
    loads[1].wait()
    for level in range(depth):
        own[level] = dot3(split(col[level]), (probe_h[...], probe_l[...]), CONTRACT_ROWS)

    peers = n_leaf - 1 + jnp.where(z > 0, 1, 0) + jnp.where(z < last, 1, 0) + jnp.where(a != z, fan, 0)
    pl.semaphore_wait(barrier, peers)

    def exchange(step):
        away = 2**step
        other = leaf + (1 - 2 * ((leaf // away) % 2)) * away
        start = sum(depth - s for s in range(step))
        return start, pltpu.make_async_remote_copy(
            src_ref=own.at[pl.ds(step, depth - step)],
            dst_ref=swap.at[pl.ds(start, depth - step)],
            send_sem=swap_send.at[step],
            recv_sem=swap_recv.at[step],
            device_id={"leaf": other, "probe": z},
            device_id_type=MESH,
        )

    def near(i):
        rows = pl.ds(pl.multiple_of(i * span, span), span)
        strips = [
            block[rows, j * span : (j + 1) * span] * mask[0, i, j].astype(jnp.float32) for j in range(side)
        ]
        app[rows, :] = dot3(
            split(jnp.concatenate(strips, axis=1)), (probe_h[...], probe_l[...]), PLAIN
        )

    done = 0
    for step in range(depth):
        start, copy = exchange(step)
        copy.start()
        if step == 0:
            loads[2].wait()
        until = side * (step + 1) // depth

        @pl.loop(done, until)
        def _(i):
            near(i)

        done = until
        copy.wait()
        sib_h[step * rank : (step + 1) * rank, :], sib_l[step * rank : (step + 1) * rank, :] = split(
            swap[start]
        )
        for level in range(step + 1, depth):
            own[level] = own[level] + swap[start + level - step]

    def ship(source, to, slot, begin, send, recv):
        rows = pl.ds(pl.multiple_of(begin, piece), piece)
        return pltpu.make_async_remote_copy(
            src_ref=source.at[rows] if source is app else source.at[slot, rows],
            dst_ref=got.at[slot, rows],
            send_sem=send.at[slot, begin // piece],
            recv_sem=recv.at[slot, begin // piece],
            device_id={"leaf": leaf, "probe": to},
            device_id_type=MESH,
        )

    def rightward(source, slot, begin):
        return ship(source, jnp.minimum(z + 1, last), slot, begin, right_send, right_recv)

    def leftward(source, slot, begin):
        return ship(source, jnp.maximum(z - 1, 0), slot, begin, left_send, left_recv)

    loads[3].wait()
    sends_right = (z < last - 1) if ends else (z < last)
    sends_left = (z > 1) if ends else (z > 0)

    def far(begin):
        rows = pl.ds(pl.multiple_of(begin, piece), piece)
        factors = jnp.concatenate([row[level, rows, :] for level in range(depth)], axis=1)
        value = app[rows, :] + dot3(split(factors), (sib_h[...], sib_l[...]), PLAIN)
        app[rows, :] = value
        app_h[rows, :], app_l[rows, :] = split(value)

    @pl.loop(0, pieces)
    def _(c):
        up, low = c * piece, half + c * piece
        far(up)

        @pl.when(sends_right)
        def _():
            rightward(app, z, up).start()

        far(low)

        @pl.when(sends_left)
        def _():
            leftward(app, z, low).start()

    if ends:
        @pl.loop(0, pieces)
        def _(c):
            @pl.when(z == 0)
            def _():
                rightward(app, z, half + c * piece).start()

            @pl.when(z == last)
            def _():
                leftward(app, z, c * piece).start()

    keep = pltpu.make_async_copy(app, app_hbm, out_sem)
    keep.start()

    def gram(slot, source, begin, fresh):
        into = pl.ds(pl.multiple_of(slot * width, width), width)
        rows = pl.ds(pl.multiple_of(begin, half), half)
        here = (app_h[rows, :], app_l[rows, :])
        there = here if source is None else split(source[slot, rows, :])
        value = dot3(there, here, CONTRACT_ROWS)
        part[into, :] = value if fresh else part[into, :] + value

    part[...] = jnp.zeros_like(part)

    @pl.loop(0, 2)
    def _(h):
        gram(z, None, h * half, False)

    @pl.loop(1, n_probe)
    def _(d):
        from_left = (z - d >= 0) & ((z < last) | (d > 1) | (not ends))
        from_right = (z + d <= last) & ((z > 0) | (d > 1) | (not ends))
        low_slot, high_slot = jnp.maximum(z - d, 0), jnp.minimum(z + d, last)

        @pl.loop(0, pieces)
        def _(c):
            up, low = c * piece, half + c * piece

            @pl.when(from_left)
            def _():
                rightward(got, low_slot, up).wait_recv()

                @pl.when(z < last)
                def _():
                    rightward(got, low_slot, up).start()

            @pl.when(from_right)
            def _():
                leftward(got, high_slot, low).wait_recv()

                @pl.when(z > 0)
                def _():
                    leftward(got, high_slot, low).start()

        @pl.loop(0, 2)
        def _(h):
            @pl.when(jnp.where(h == 0, from_left, from_right))
            def _():
                gram(jnp.where(h == 0, low_slot, high_slot), got, h * half, False)

    if ends:
        at_low, at_high = z == 1, z == last - 1

        @pl.loop(0, pieces)
        def _(c):
            @pl.when(at_low)
            def _():
                rightward(got, z - 1, half + c * piece).wait_recv()

            @pl.when(at_high)
            def _():
                leftward(got, z + 1, c * piece).wait_recv()

        @pl.loop(0, 2)
        def _(h):
            @pl.when(jnp.where(h == 0, at_high, at_low))
            def _():
                gram(jnp.where(h == 0, jnp.minimum(z + 1, last), jnp.maximum(z - 1, 0)), got, h * half, False)

    def share(k):
        to = (leaf + k) % n_leaf
        return pltpu.make_async_remote_copy(
            src_ref=part.at[pl.ds(pl.multiple_of(to * slab, slab), slab)],
            dst_ref=shares.at[k],
            send_sem=share_send.at[k],
            recv_sem=share_recv.at[k],
            device_id={"leaf": to, "probe": z},
            device_id_type=MESH,
        )

    @pl.loop(1, n_leaf)
    def _(k):
        share(k).start()

    total[...] = part[pl.ds(pl.multiple_of(leaf * slab, slab), slab), :]

    @pl.loop(1, n_leaf)
    def _(k):
        share(k).wait_recv()
        total[...] = total[...] + shares[k]

    scale = 1.0 / (points * n_leaf)

    def trade(c):
        return pltpu.make_async_remote_copy(
            src_ref=total,
            dst_ref=extra.at[pl.ds(pl.multiple_of(b * slab, slab), slab)],
            send_sem=extra_send.at[c],
            recv_sem=extra_recv.at[b],
            device_id={"leaf": z * fan + c, "probe": a},
            device_id_type=MESH,
        )

    def traded(c):
        return pltpu.make_async_remote_copy(
            src_ref=total,
            dst_ref=extra.at[pl.ds(pl.multiple_of(c * slab, slab), slab)],
            send_sem=extra_send.at[c],
            recv_sem=extra_recv.at[c],
            device_id={"leaf": z * fan + c, "probe": a},
            device_id_type=MESH,
        )

    @pl.when(a != z)
    def _():
        @pl.loop(0, fan)
        def _(c):
            trade(c).start()

        @pl.loop(0, fan)
        def _(c):
            traded(c).wait_recv()

        turned[...] = extra[...].T
        gram_ref[...] = (total[...] + turned[pl.ds(pl.multiple_of(b * slab, slab), slab), :]) * scale

        @pl.loop(0, fan)
        def _(c):
            trade(c).wait_send()

    @pl.when(a == z)
    def _():
        gram_ref[...] = total[...] * scale

    @pl.loop(0, pieces)
    def _(c):
        up, low = c * piece, half + c * piece

        @pl.when(sends_right)
        def _():
            rightward(app, z, up).wait_send()

        @pl.when(sends_left)
        def _():
            leftward(app, z, low).wait_send()

        if ends:

            @pl.when(z == 0)
            def _():
                rightward(app, z, low).wait_send()

            @pl.when(z == last)
            def _():
                leftward(app, z, up).wait_send()

        @pl.loop(1, n_probe)
        def _(d):
            @pl.when((z - d >= 0) & (z < last))
            def _():
                rightward(got, jnp.maximum(z - d, 0), up).wait_send()

            @pl.when((z + d <= last) & (z > 0))
            def _():
                leftward(got, jnp.minimum(z + d, last), low).wait_send()

    @pl.loop(1, n_leaf)
    def _(k):
        share(k).wait_send()

    keep.wait()


def local(n_leaf, n_probe, leaf_blocks, block_mask, row_factor_stack, column_factor_stack, probes):
    depth, points, rank = row_factor_stack.shape
    width = probes.shape[1]
    slab = n_probe * width // n_leaf
    fan = n_leaf // n_probe
    pieces = 4
    f32, bf16 = jnp.float32, jnp.bfloat16
    dma = pltpu.SemaphoreType.DMA
    hbm = pl.BlockSpec(memory_space=pl.ANY)
    return pl.pallas_call(
        functools.partial(kernel, n_leaf, n_probe, pieces),
        out_shape=(
            jax.ShapeDtypeStruct((points, width), f32),
            jax.ShapeDtypeStruct((slab, width), f32),
        ),
        in_specs=[pl.BlockSpec(memory_space=pltpu.SMEM), hbm, hbm, hbm, hbm],
        out_specs=(hbm, pl.BlockSpec(memory_space=pltpu.VMEM)),
        scratch_shapes=[
            pltpu.VMEM((points, points), f32),
            pltpu.VMEM((depth, points, rank), f32),
            pltpu.VMEM((depth, points, rank), f32),
            pltpu.VMEM((points, width), f32),
            pltpu.VMEM((points, width), bf16),
            pltpu.VMEM((points, width), bf16),
            pltpu.VMEM((depth, rank, width), f32),
            pltpu.VMEM((depth * (depth + 1) // 2, rank, width), f32),
            pltpu.VMEM((depth * rank, width), bf16),
            pltpu.VMEM((depth * rank, width), bf16),
            pltpu.VMEM((points, width), f32),
            pltpu.VMEM((points, width), bf16),
            pltpu.VMEM((points, width), bf16),
            pltpu.VMEM((n_probe, points, width), f32),
            pltpu.VMEM((n_probe * width, width), f32),
            pltpu.VMEM((n_leaf, slab, width), f32),
            pltpu.VMEM((slab, width), f32),
            pltpu.VMEM((width, width), f32),
            pltpu.VMEM((width, width), f32),
            dma((4,)),
            dma,
            dma((depth,)),
            dma((depth,)),
            dma((n_probe, 2 * pieces)),
            dma((n_probe, 2 * pieces)),
            dma((n_probe, 2 * pieces)),
            dma((n_probe, 2 * pieces)),
            dma((n_leaf,)),
            dma((n_leaf,)),
            dma((fan,)),
            dma((fan,)),
        ],
        compiler_params=pltpu.CompilerParams(
            collective_id=0, has_side_effects=True, vmem_limit_bytes=48 * 2**20
        ),
    )(block_mask, leaf_blocks, row_factor_stack, column_factor_stack, probes)


def solution(mesh):
    return jax.shard_map(
        functools.partial(local, mesh.shape["leaf"], mesh.shape["probe"]),
        mesh=mesh,
        in_specs=(
            P("leaf", None),
            P("leaf", None, None),
            P(None, "leaf", None),
            P(None, "leaf", None),
            P("leaf", "probe"),
        ),
        out_specs=(P("leaf", "probe"), P("leaf", "probe")),
        check_vma=False,
    )
```

```python
import functools

import jax
import jax.numpy as jnp
from jax import lax
from jax.experimental import pallas as pl
from jax.experimental.pallas import tpu as pltpu
from jax.sharding import PartitionSpec as P

MESH = pl.DeviceIdType.MESH
CONTRACT_ROWS = (((0,), (0,)), ((), ()))
PLAIN = (((1,), (0,)), ((), ()))


def split(value):
    high = value.astype(jnp.bfloat16)
    return high, (value - high.astype(jnp.float32)).astype(jnp.bfloat16)


def dot3(left, right, dims):
    (lh, ll), (rh, rl) = left, right
    dot = functools.partial(lax.dot_general, dimension_numbers=dims, preferred_element_type=jnp.float32)
    return dot(lh, rh) + (dot(lh, rl) + dot(ll, rh))


def kernel(
    n_leaf, n_probe, pieces,
    mask, block_hbm, row_hbm, col_hbm, probe_hbm, app_hbm, gram_ref,
    block, row, col, probe, probe_h, probe_l, own, swap, sib_h, sib_l,
    app, app_h, app_l, got, part, shares, total, extra, turned, kept_h, kept_l,
    load_sem, out_sem, swap_send, swap_recv, right_send, right_recv, left_send, left_recv,
    share_send, share_recv, extra_send, extra_recv,
):
    depth, rank = row.shape[0], row.shape[2]
    points, width = app.shape
    side = mask.shape[1]
    span = points // side
    half = points // 2
    piece = half // pieces
    leaf, z = lax.axis_index("leaf"), lax.axis_index("probe")
    slab = n_probe * width // n_leaf
    fan = n_leaf // n_probe
    a, b = leaf // fan, leaf % fan
    last = n_probe - 1
    ends = n_probe > 2

    loads = [
        pltpu.make_async_copy(source, target, load_sem.at[i])
        for i, (source, target) in enumerate(
            ((probe_hbm, probe), (col_hbm, col), (block_hbm, block), (row_hbm, row))
        )
    ]
    for load in loads:
        load.start()

    barrier = pltpu.get_barrier_semaphore()

    @pl.loop(1, n_leaf)
    def _(k):
        pl.semaphore_signal(
            barrier, inc=1, device_id={"leaf": (leaf + k) % n_leaf, "probe": z}, device_id_type=MESH
        )

    @pl.when(z > 0)
    def _():
        pl.semaphore_signal(barrier, inc=1, device_id={"leaf": leaf, "probe": z - 1}, device_id_type=MESH)

    @pl.when(z < last)
    def _():
        pl.semaphore_signal(barrier, inc=1, device_id={"leaf": leaf, "probe": z + 1}, device_id_type=MESH)

    @pl.when(a != z)
    def _():
        @pl.loop(0, fan)
        def _(c):
            pl.semaphore_signal(
                barrier, inc=1, device_id={"leaf": z * fan + c, "probe": a}, device_id_type=MESH
            )

    loads[0].wait()
    ph, plo = split(probe[...])
    probe_h[...] = ph
    probe_l[...] = plo
    loads[1].wait()
    columns = jnp.concatenate([col[level] for level in range(depth)], axis=1)
    own[...] = dot3(split(columns), (probe_h[...], probe_l[...]), CONTRACT_ROWS).reshape(own.shape)

    peers = n_leaf - 1 + jnp.where(z > 0, 1, 0) + jnp.where(z < last, 1, 0) + jnp.where(a != z, fan, 0)
    pl.semaphore_wait(barrier, peers)

    def exchange(step):
        away = 2**step
        other = leaf + (1 - 2 * ((leaf // away) % 2)) * away
        start = sum(depth - s for s in range(step))
        return start, pltpu.make_async_remote_copy(
            src_ref=own.at[pl.ds(step, depth - step)],
            dst_ref=swap.at[pl.ds(start, depth - step)],
            send_sem=swap_send.at[step],
            recv_sem=swap_recv.at[step],
            device_id={"leaf": other, "probe": z},
            device_id_type=MESH,
        )

    def near(which):
        @pl.loop(0, side // 2)
        def _(i):
            line = which * (side // 2) + i
            rows = pl.ds(pl.multiple_of(line * span, span), span)
            strips = [
                block[rows, j * span : (j + 1) * span] * mask[0, line, j].astype(jnp.float32)
                for j in range(side)
            ]
            into = pl.ds(pl.multiple_of(i * span, span), span)
            kept_h[into, :], kept_l[into, :] = split(jnp.concatenate(strips, axis=1))

        app[which * half : (which + 1) * half, :] = dot3(
            (kept_h[...], kept_l[...]), (probe_h[...], probe_l[...]), PLAIN
        )

    for step in range(depth):
        start, copy = exchange(step)
        copy.start()
        if step == 0:
            loads[2].wait()
        for which in range(2):
            if step == min(which, depth - 1):
                near(which)
        copy.wait()
        sib_h[step * rank : (step + 1) * rank, :], sib_l[step * rank : (step + 1) * rank, :] = split(
            swap[start]
        )
        for level in range(step + 1, depth):
            own[level] = own[level] + swap[start + level - step]

    def ship(source, to, slot, begin, send, recv):
        rows = pl.ds(pl.multiple_of(begin, piece), piece)
        return pltpu.make_async_remote_copy(
            src_ref=source.at[rows] if source is app else source.at[slot, rows],
            dst_ref=got.at[slot, rows],
            send_sem=send.at[slot, begin // piece],
            recv_sem=recv.at[slot, begin // piece],
            device_id={"leaf": leaf, "probe": to},
            device_id_type=MESH,
        )

    def rightward(source, slot, begin):
        return ship(source, jnp.minimum(z + 1, last), slot, begin, right_send, right_recv)

    def leftward(source, slot, begin):
        return ship(source, jnp.maximum(z - 1, 0), slot, begin, left_send, left_recv)

    loads[3].wait()
    sends_right = (z < last - 1) if ends else (z < last)
    sends_left = (z > 1) if ends else (z > 0)

    def far(which):
        rows = slice(which * half, (which + 1) * half)
        factors = jnp.concatenate([row[level, rows, :] for level in range(depth)], axis=1)
        value = app[rows, :] + dot3(split(factors), (sib_h[...], sib_l[...]), PLAIN)
        app[rows, :] = value
        app_h[rows, :], app_l[rows, :] = split(value)

    far(0)

    @pl.when(sends_right)
    def _():
        @pl.loop(0, pieces)
        def _(c):
            rightward(app, z, c * piece).start()

    far(1)

    @pl.when(sends_left)
    def _():
        @pl.loop(0, pieces)
        def _(c):
            leftward(app, z, half + c * piece).start()

    if ends:
        @pl.loop(0, pieces)
        def _(c):
            @pl.when(z == 0)
            def _():
                rightward(app, z, half + c * piece).start()

            @pl.when(z == last)
            def _():
                leftward(app, z, c * piece).start()

    keep = pltpu.make_async_copy(app, app_hbm, out_sem)
    keep.start()

    def gram(slot, source, begin, fresh):
        into = pl.ds(pl.multiple_of(slot * width, width), width)
        rows = pl.ds(pl.multiple_of(begin, half), half)
        here = (app_h[rows, :], app_l[rows, :])
        there = here if source is None else split(source[slot, rows, :])
        value = dot3(there, here, CONTRACT_ROWS)
        part[into, :] = value if fresh else part[into, :] + value

    def share(k):
        to = (leaf + k) % n_leaf
        return pltpu.make_async_remote_copy(
            src_ref=part.at[pl.ds(pl.multiple_of(to * slab, slab), slab)],
            dst_ref=shares.at[k],
            send_sem=share_send.at[k],
            recv_sem=share_recv.at[k],
            device_id={"leaf": to, "probe": z},
            device_id_type=MESH,
        )

    def give(slot):
        @pl.loop(0, fan)
        def _(c):
            to = slot * fan + c

            @pl.when(to != leaf)
            def _():
                share((to - leaf + n_leaf) % n_leaf).start()

    part[...] = jnp.zeros_like(part)

    @pl.loop(0, 2)
    def _(h):
        gram(z, None, h * half, False)

    give(z)

    @pl.loop(1, n_probe)
    def _(d):
        from_left = (z - d >= 0) & ((z < last) | (d > 1) | (not ends))
        from_right = (z + d <= last) & ((z > 0) | (d > 1) | (not ends))
        low_slot, high_slot = jnp.maximum(z - d, 0), jnp.minimum(z + d, last)

        @pl.loop(0, pieces)
        def _(c):
            up, low = c * piece, half + c * piece

            @pl.when(from_left)
            def _():
                rightward(got, low_slot, up).wait_recv()

                @pl.when(z < last)
                def _():
                    rightward(got, low_slot, up).start()

            @pl.when(from_right)
            def _():
                leftward(got, high_slot, low).wait_recv()

                @pl.when(z > 0)
                def _():
                    leftward(got, high_slot, low).start()

        @pl.loop(0, 2)
        def _(h):
            @pl.when(jnp.where(h == 0, from_left, from_right))
            def _():
                slot = jnp.where(h == 0, low_slot, high_slot)
                gram(slot, got, h * half, False)
                whole = (d > 1) | jnp.where(h == 0, z != 1, z != last - 1) | (not ends)

                @pl.when(whole)
                def _():
                    give(slot)

    if ends:
        at_low, at_high = z == 1, z == last - 1

        @pl.loop(0, pieces)
        def _(c):
            @pl.when(at_low)
            def _():
                rightward(got, z - 1, half + c * piece).wait_recv()

            @pl.when(at_high)
            def _():
                leftward(got, z + 1, c * piece).wait_recv()

        @pl.loop(0, 2)
        def _(h):
            @pl.when(jnp.where(h == 0, at_high, at_low))
            def _():
                slot = jnp.where(h == 0, jnp.minimum(z + 1, last), jnp.maximum(z - 1, 0))
                gram(slot, got, h * half, False)
                give(slot)

    total[...] = part[pl.ds(pl.multiple_of(leaf * slab, slab), slab), :]

    def holds(slot):
        return (not ends) | (((z > 0) | (slot != 1)) & ((z < last) | (slot != last - 1)))

    @pl.when(holds(a))
    def _():
        @pl.loop(1, n_leaf)
        def _(k):
            share(k).wait_recv()
            total[...] = total[...] + shares[k]

    scale = 1.0 / (points * n_leaf)

    tile = extra.shape[1]

    def trade(c, at):
        return pltpu.make_async_remote_copy(
            src_ref=total if tile == width else total.at[:, pl.ds(pl.multiple_of(c * tile, tile), tile)],
            dst_ref=extra.at[pl.ds(pl.multiple_of(at * slab, slab), slab)],
            send_sem=extra_send.at[c],
            recv_sem=extra_recv.at[at],
            device_id={"leaf": z * fan + c, "probe": a},
            device_id_type=MESH,
        )

    @pl.when(a != z)
    def _():
        @pl.loop(0, fan)
        def _(c):
            trade(c, b).start()

        @pl.loop(0, fan)
        def _(c):
            trade(c, c).wait_recv()

        turned[...] = extra[...].T
        skip = 0 if tile == slab else pl.multiple_of(b * slab, slab)
        gram_ref[...] = (total[...] + turned[pl.ds(skip, slab), :]) * scale

        @pl.loop(0, fan)
        def _(c):
            trade(c, b).wait_send()

    @pl.when(a == z)
    def _():
        gram_ref[...] = total[...] * scale

    @pl.loop(0, pieces)
    def _(c):
        up, low = c * piece, half + c * piece

        @pl.when(sends_right)
        def _():
            rightward(app, z, up).wait_send()

        @pl.when(sends_left)
        def _():
            leftward(app, z, low).wait_send()

        if ends:

            @pl.when(z == 0)
            def _():
                rightward(app, z, low).wait_send()

            @pl.when(z == last)
            def _():
                leftward(app, z, up).wait_send()

        @pl.loop(1, n_probe)
        def _(d):
            @pl.when((z - d >= 0) & (z < last))
            def _():
                rightward(got, jnp.maximum(z - d, 0), up).wait_send()

            @pl.when((z + d <= last) & (z > 0))
            def _():
                leftward(got, jnp.minimum(z + d, last), low).wait_send()

    @pl.loop(1, n_leaf)
    def _(k):
        @pl.when(holds(((leaf + k) % n_leaf) // fan))
        def _():
            share(k).wait_send()

    keep.wait()


def local(n_leaf, n_probe, leaf_blocks, block_mask, row_factor_stack, column_factor_stack, probes):
    depth, points, rank = row_factor_stack.shape
    width = probes.shape[1]
    slab = n_probe * width // n_leaf
    fan = n_leaf // n_probe
    pieces = 4
    tile = slab if slab % 128 == 0 else width
    f32, bf16 = jnp.float32, jnp.bfloat16
    dma = pltpu.SemaphoreType.DMA
    hbm = pl.BlockSpec(memory_space=pltpu.HBM)
    return pl.pallas_call(
        functools.partial(kernel, n_leaf, n_probe, pieces),
        out_shape=(
            jax.ShapeDtypeStruct((points, width), f32),
            jax.ShapeDtypeStruct((slab, width), f32),
        ),
        in_specs=[pl.BlockSpec(memory_space=pltpu.SMEM), hbm, hbm, hbm, hbm],
        out_specs=(hbm, pl.BlockSpec(memory_space=pltpu.VMEM)),
        scratch_shapes=[
            pltpu.VMEM((points, points), f32),
            pltpu.VMEM((depth, points, rank), f32),
            pltpu.VMEM((depth, points, rank), f32),
            pltpu.VMEM((points, width), f32),
            pltpu.VMEM((points, width), bf16),
            pltpu.VMEM((points, width), bf16),
            pltpu.VMEM((depth, rank, width), f32),
            pltpu.VMEM((depth * (depth + 1) // 2, rank, width), f32),
            pltpu.VMEM((depth * rank, width), bf16),
            pltpu.VMEM((depth * rank, width), bf16),
            pltpu.VMEM((points, width), f32),
            pltpu.VMEM((points, width), bf16),
            pltpu.VMEM((points, width), bf16),
            pltpu.VMEM((n_probe, points, width), f32),
            pltpu.VMEM((n_probe * width, width), f32),
            pltpu.VMEM((n_leaf, slab, width), f32),
            pltpu.VMEM((slab, width), f32),
            pltpu.VMEM((width, tile), f32),
            pltpu.VMEM((tile, width), f32),
            pltpu.VMEM((points // 2, points), bf16),
            pltpu.VMEM((points // 2, points), bf16),
            dma((4,)),
            dma,
            dma((depth,)),
            dma((depth,)),
            dma((n_probe, 2 * pieces)),
            dma((n_probe, 2 * pieces)),
            dma((n_probe, 2 * pieces)),
            dma((n_probe, 2 * pieces)),
            dma((n_leaf,)),
            dma((n_leaf,)),
            dma((fan,)),
            dma((fan,)),
        ],
        compiler_params=pltpu.CompilerParams(
            collective_id=0, has_side_effects=True, vmem_limit_bytes=67043328
        ),
    )(block_mask, leaf_blocks, row_factor_stack, column_factor_stack, probes)


def solution(mesh):
    return jax.shard_map(
        functools.partial(local, mesh.shape["leaf"], mesh.shape["probe"]),
        mesh=mesh,
        in_specs=(
            P("leaf", None),
            P("leaf", None, None),
            P(None, "leaf", None),
            P(None, "leaf", None),
            P("leaf", "probe"),
        ),
        out_specs=(P("leaf", "probe"), P("leaf", "probe")),
        check_vma=False,
    )
```

```python
import functools

import jax
import jax.numpy as jnp
from jax import lax
from jax.experimental import pallas as pl
from jax.experimental.pallas import tpu as pltpu
from jax.sharding import PartitionSpec as P

MESH = pl.DeviceIdType.MESH
CONTRACT_ROWS = (((0,), (0,)), ((), ()))
PLAIN = (((1,), (0,)), ((), ()))


def split(value):
    high = value.astype(jnp.bfloat16)
    return high, (value - high.astype(jnp.float32)).astype(jnp.bfloat16)


def dot3(left, right, dims):
    (lh, ll), (rh, rl) = left, right
    dot = functools.partial(lax.dot_general, dimension_numbers=dims, preferred_element_type=jnp.float32)
    return dot(lh, rh) + (dot(lh, rl) + dot(ll, rh))


def kernel(
    n_leaf, n_probe, pieces,
    mask, block_hbm, row_hbm, col_hbm, probe_hbm, app_hbm, gram_ref,
    block, row, col, probe, probe_h, probe_l, own, swap, rest, sib_h, sib_l,
    app, app_h, app_l, got, part, shares, total, extra, turned, kept_h, kept_l,
    load_sem, out_sem, swap_send, swap_recv, rest_send, rest_recv, right_send, right_recv, left_send, left_recv,
    share_send, share_recv, extra_send, extra_recv,
):
    depth, rank = row.shape[0], row.shape[2]
    points, width = app.shape
    side = mask.shape[1]
    span = points // side
    half = points // 2
    piece = half // pieces
    leaf, z = lax.axis_index("leaf"), lax.axis_index("probe")
    slab = n_probe * width // n_leaf
    fan = n_leaf // n_probe
    a, b = leaf // fan, leaf % fan
    last = n_probe - 1
    ends = n_probe > 2

    loads = [
        pltpu.make_async_copy(source, target, load_sem.at[i])
        for i, (source, target) in enumerate(
            ((probe_hbm, probe), (col_hbm, col), (block_hbm, block), (row_hbm, row))
        )
    ]
    loads[0].start()
    loads[1].start()

    barrier = pltpu.get_barrier_semaphore()

    @pl.loop(1, n_leaf)
    def _(k):
        pl.semaphore_signal(
            barrier, inc=1, device_id={"leaf": (leaf + k) % n_leaf, "probe": z}, device_id_type=MESH
        )

    @pl.when(z > 0)
    def _():
        pl.semaphore_signal(barrier, inc=1, device_id={"leaf": leaf, "probe": z - 1}, device_id_type=MESH)

    @pl.when(z < last)
    def _():
        pl.semaphore_signal(barrier, inc=1, device_id={"leaf": leaf, "probe": z + 1}, device_id_type=MESH)

    @pl.when(a != z)
    def _():
        @pl.loop(0, fan)
        def _(c):
            pl.semaphore_signal(
                barrier, inc=1, device_id={"leaf": z * fan + c, "probe": a}, device_id_type=MESH
            )

    loads[0].wait()
    ph, plo = split(probe[...])
    probe_h[...] = ph
    probe_l[...] = plo
    loads[1].wait()
    loads[2].start()
    loads[3].start()
    columns = jnp.concatenate([col[level] for level in range(depth)], axis=1)
    projected = dot3(split(columns), (probe_h[...], probe_l[...]), CONTRACT_ROWS)
    strip = own.shape[3]
    for side_half in range(2):
        own[side_half] = projected[:, side_half * strip : (side_half + 1) * strip].reshape(own.shape[1:])

    peers = n_leaf - 1 + jnp.where(z > 0, 1, 0) + jnp.where(z < last, 1, 0) + jnp.where(a != z, fan, 0)
    pl.semaphore_wait(barrier, peers)

    mine = leaf % 2
    mate = leaf + 1 - 2 * mine

    def exchange(step):
        away = 2**step
        other = leaf + (1 - 2 * ((leaf // away) % 2)) * away
        start = sum(depth - s for s in range(step))
        return start, pltpu.make_async_remote_copy(
            src_ref=own.at[1 - mine if step == 0 else mine, pl.ds(step, depth - step)],
            dst_ref=swap.at[pl.ds(start, depth - step)],
            send_sem=swap_send.at[step],
            recv_sem=swap_recv.at[step],
            device_id={"leaf": other, "probe": z},
            device_id_type=MESH,
        )

    def complete(level):
        return pltpu.make_async_remote_copy(
            src_ref=own.at[mine, 0] if level == 0 else swap.at[sum(depth - s for s in range(level))],
            dst_ref=rest.at[level],
            send_sem=rest_send.at[level],
            recv_sem=rest_recv.at[level],
            device_id={"leaf": mate, "probe": z},
            device_id_type=MESH,
        )

    def near(which):
        @pl.loop(0, side // 2)
        def _(i):
            line = which * (side // 2) + i
            rows = pl.ds(pl.multiple_of(line * span, span), span)
            strips = [
                block[rows, j * span : (j + 1) * span] * mask[0, line, j].astype(jnp.float32)
                for j in range(side)
            ]
            into = pl.ds(pl.multiple_of(i * span, span), span)
            kept_h[into, :], kept_l[into, :] = split(jnp.concatenate(strips, axis=1))

        app[which * half : (which + 1) * half, :] = dot3(
            (kept_h[...], kept_l[...]), (probe_h[...], probe_l[...]), PLAIN
        )

    def sibling(level, which, value):
        rows, lanes = slice(level * rank, (level + 1) * rank), pl.ds(pl.multiple_of(which * strip, strip), strip)
        sib_h[rows, lanes], sib_l[rows, lanes] = split(value)

    for step in range(depth):
        start, copy = exchange(step)
        copy.start()
        if step == 0:
            complete(0).start()
            loads[2].wait()
        for which in range(2):
            if step == min(which, depth - 1):
                near(which)
        copy.wait()
        if step > 0:
            complete(step).start()
        for level in range(step + 1, depth):
            own[mine, level] = own[mine, level] + swap[start + level - step]
        sibling(step, mine, swap[start])
    for level in range(depth):
        complete(level).wait()
        sibling(level, 1 - mine, rest[level])

    def ship(source, to, slot, begin, send, recv):
        rows = pl.ds(pl.multiple_of(begin, piece), piece)
        return pltpu.make_async_remote_copy(
            src_ref=source.at[rows] if source is app else source.at[slot, rows],
            dst_ref=got.at[slot, rows],
            send_sem=send.at[slot, begin // piece],
            recv_sem=recv.at[slot, begin // piece],
            device_id={"leaf": leaf, "probe": to},
            device_id_type=MESH,
        )

    def rightward(source, slot, begin):
        return ship(source, jnp.minimum(z + 1, last), slot, begin, right_send, right_recv)

    def leftward(source, slot, begin):
        return ship(source, jnp.maximum(z - 1, 0), slot, begin, left_send, left_recv)

    loads[3].wait()
    sends_right = (z < last - 1) if ends else (z < last)
    sends_left = (z > 1) if ends else (z > 0)

    def far(which):
        rows = slice(which * half, (which + 1) * half)
        factors = jnp.concatenate([row[level, rows, :] for level in range(depth)], axis=1)
        value = app[rows, :] + dot3(split(factors), (sib_h[...], sib_l[...]), PLAIN)
        app[rows, :] = value
        app_h[rows, :], app_l[rows, :] = split(value)

    far(0)

    @pl.when(sends_right)
    def _():
        @pl.loop(0, pieces)
        def _(c):
            rightward(app, z, c * piece).start()

    far(1)

    @pl.when(sends_left)
    def _():
        @pl.loop(0, pieces)
        def _(c):
            leftward(app, z, half + c * piece).start()

    if ends:
        @pl.loop(0, pieces)
        def _(c):
            @pl.when(z == 0)
            def _():
                rightward(app, z, half + c * piece).start()

            @pl.when(z == last)
            def _():
                leftward(app, z, c * piece).start()

    keep = pltpu.make_async_copy(app, app_hbm, out_sem)
    keep.start()

    def gram(slot, source, begin, fresh):
        into = pl.ds(pl.multiple_of(slot * width, width), width)
        rows = pl.ds(pl.multiple_of(begin, half), half)
        here = (app_h[rows, :], app_l[rows, :])
        there = here if source is None else split(source[slot, rows, :])
        value = dot3(there, here, CONTRACT_ROWS)
        part[into, :] = value if fresh else part[into, :] + value

    def share(k):
        to = (leaf + k) % n_leaf
        return pltpu.make_async_remote_copy(
            src_ref=part.at[pl.ds(pl.multiple_of(to * slab, slab), slab)],
            dst_ref=shares.at[k],
            send_sem=share_send.at[k],
            recv_sem=share_recv.at[k],
            device_id={"leaf": to, "probe": z},
            device_id_type=MESH,
        )

    def give(slot):
        @pl.loop(0, fan)
        def _(c):
            to = slot * fan + c

            @pl.when(to != leaf)
            def _():
                share((to - leaf + n_leaf) % n_leaf).start()

    part[...] = jnp.zeros_like(part)

    @pl.loop(0, 2)
    def _(h):
        gram(z, None, h * half, False)

    give(z)

    @pl.loop(1, n_probe)
    def _(d):
        from_left = (z - d >= 0) & ((z < last) | (d > 1) | (not ends))
        from_right = (z + d <= last) & ((z > 0) | (d > 1) | (not ends))
        low_slot, high_slot = jnp.maximum(z - d, 0), jnp.minimum(z + d, last)

        @pl.loop(0, pieces)
        def _(c):
            up, low = c * piece, half + c * piece

            @pl.when(from_left)
            def _():
                rightward(got, low_slot, up).wait_recv()

                @pl.when(z < last)
                def _():
                    rightward(got, low_slot, up).start()

            @pl.when(from_right)
            def _():
                leftward(got, high_slot, low).wait_recv()

                @pl.when(z > 0)
                def _():
                    leftward(got, high_slot, low).start()

        @pl.loop(0, 2)
        def _(h):
            @pl.when(jnp.where(h == 0, from_left, from_right))
            def _():
                slot = jnp.where(h == 0, low_slot, high_slot)
                gram(slot, got, h * half, False)
                whole = (d > 1) | jnp.where(h == 0, z != 1, z != last - 1) | (not ends)

                @pl.when(whole)
                def _():
                    give(slot)

    if ends:
        at_low, at_high = z == 1, z == last - 1

        @pl.loop(0, pieces)
        def _(c):
            @pl.when(at_low)
            def _():
                rightward(got, z - 1, half + c * piece).wait_recv()

            @pl.when(at_high)
            def _():
                leftward(got, z + 1, c * piece).wait_recv()

        @pl.loop(0, 2)
        def _(h):
            @pl.when(jnp.where(h == 0, at_high, at_low))
            def _():
                slot = jnp.where(h == 0, jnp.minimum(z + 1, last), jnp.maximum(z - 1, 0))
                gram(slot, got, h * half, False)
                give(slot)

    total[...] = part[pl.ds(pl.multiple_of(leaf * slab, slab), slab), :]

    def holds(slot):
        return (not ends) | (((z > 0) | (slot != 1)) & ((z < last) | (slot != last - 1)))

    @pl.when(holds(a))
    def _():
        @pl.loop(1, n_leaf)
        def _(k):
            share(k).wait_recv()
            total[...] = total[...] + shares[k]

    scale = 1.0 / (points * n_leaf)

    tile = extra.shape[1]

    def trade(c, at):
        return pltpu.make_async_remote_copy(
            src_ref=total if tile == width else total.at[:, pl.ds(pl.multiple_of(c * tile, tile), tile)],
            dst_ref=extra.at[pl.ds(pl.multiple_of(at * slab, slab), slab)],
            send_sem=extra_send.at[c],
            recv_sem=extra_recv.at[at],
            device_id={"leaf": z * fan + c, "probe": a},
            device_id_type=MESH,
        )

    @pl.when(a != z)
    def _():
        @pl.loop(0, fan)
        def _(c):
            trade(c, b).start()

        @pl.loop(0, fan)
        def _(c):
            trade(c, c).wait_recv()

        turned[...] = extra[...].T
        skip = 0 if tile == slab else pl.multiple_of(b * slab, slab)
        gram_ref[...] = (total[...] + turned[pl.ds(skip, slab), :]) * scale

        @pl.loop(0, fan)
        def _(c):
            trade(c, b).wait_send()

    @pl.when(a == z)
    def _():
        gram_ref[...] = total[...] * scale

    @pl.loop(0, pieces)
    def _(c):
        up, low = c * piece, half + c * piece

        @pl.when(sends_right)
        def _():
            rightward(app, z, up).wait_send()

        @pl.when(sends_left)
        def _():
            leftward(app, z, low).wait_send()

        if ends:

            @pl.when(z == 0)
            def _():
                rightward(app, z, low).wait_send()

            @pl.when(z == last)
            def _():
                leftward(app, z, up).wait_send()

        @pl.loop(1, n_probe)
        def _(d):
            @pl.when((z - d >= 0) & (z < last))
            def _():
                rightward(got, jnp.maximum(z - d, 0), up).wait_send()

            @pl.when((z + d <= last) & (z > 0))
            def _():
                leftward(got, jnp.minimum(z + d, last), low).wait_send()

    @pl.loop(1, n_leaf)
    def _(k):
        @pl.when(holds(((leaf + k) % n_leaf) // fan))
        def _():
            share(k).wait_send()

    keep.wait()


def local(n_leaf, n_probe, leaf_blocks, block_mask, row_factor_stack, column_factor_stack, probes):
    depth, points, rank = row_factor_stack.shape
    width = probes.shape[1]
    slab = n_probe * width // n_leaf
    fan = n_leaf // n_probe
    pieces = 4
    tile = slab if slab % 128 == 0 else width
    f32, bf16 = jnp.float32, jnp.bfloat16
    dma = pltpu.SemaphoreType.DMA
    hbm = pl.BlockSpec(memory_space=pltpu.HBM)
    return pl.pallas_call(
        functools.partial(kernel, n_leaf, n_probe, pieces),
        out_shape=(
            jax.ShapeDtypeStruct((points, width), f32),
            jax.ShapeDtypeStruct((slab, width), f32),
        ),
        in_specs=[pl.BlockSpec(memory_space=pltpu.SMEM), hbm, hbm, hbm, hbm],
        out_specs=(hbm, pl.BlockSpec(memory_space=pltpu.VMEM)),
        scratch_shapes=[
            pltpu.VMEM((points, points), f32),
            pltpu.VMEM((depth, points, rank), f32),
            pltpu.VMEM((depth, points, rank), f32),
            pltpu.VMEM((points, width), f32),
            pltpu.VMEM((points, width), bf16),
            pltpu.VMEM((points, width), bf16),
            pltpu.VMEM((2, depth, rank, width // 2), f32),
            pltpu.VMEM((depth * (depth + 1) // 2, rank, width // 2), f32),
            pltpu.VMEM((depth, rank, width // 2), f32),
            pltpu.VMEM((depth * rank, width), bf16),
            pltpu.VMEM((depth * rank, width), bf16),
            pltpu.VMEM((points, width), f32),
            pltpu.VMEM((points, width), bf16),
            pltpu.VMEM((points, width), bf16),
            pltpu.VMEM((n_probe, points, width), f32),
            pltpu.VMEM((n_probe * width, width), f32),
            pltpu.VMEM((n_leaf, slab, width), f32),
            pltpu.VMEM((slab, width), f32),
            pltpu.VMEM((width, tile), f32),
            pltpu.VMEM((tile, width), f32),
            pltpu.VMEM((points // 2, points), bf16),
            pltpu.VMEM((points // 2, points), bf16),
            dma((4,)),
            dma,
            dma((depth,)),
            dma((depth,)),
            dma((depth,)),
            dma((depth,)),
            dma((n_probe, 2 * pieces)),
            dma((n_probe, 2 * pieces)),
            dma((n_probe, 2 * pieces)),
            dma((n_probe, 2 * pieces)),
            dma((n_leaf,)),
            dma((n_leaf,)),
            dma((fan,)),
            dma((fan,)),
        ],
        compiler_params=pltpu.CompilerParams(
            collective_id=0, has_side_effects=True, vmem_limit_bytes=67043328
        ),
    )(block_mask, leaf_blocks, row_factor_stack, column_factor_stack, probes)


def solution(mesh):
    return jax.shard_map(
        functools.partial(local, mesh.shape["leaf"], mesh.shape["probe"]),
        mesh=mesh,
        in_specs=(
            P("leaf", None),
            P("leaf", None, None),
            P(None, "leaf", None),
            P(None, "leaf", None),
            P("leaf", "probe"),
        ),
        out_specs=(P("leaf", "probe"), P("leaf", "probe")),
        check_vma=False,
    )
```

```python
import functools

import jax
import jax.numpy as jnp
from jax import lax
from jax.experimental import pallas as pl
from jax.experimental.pallas import tpu as pltpu
from jax.sharding import PartitionSpec as P

MESH = pl.DeviceIdType.MESH
CONTRACT_ROWS = (((0,), (0,)), ((), ()))
PLAIN = (((1,), (0,)), ((), ()))


def split(value):
    high = value.astype(jnp.bfloat16)
    return high, (value - high.astype(jnp.float32)).astype(jnp.bfloat16)


def dot3(left, right, dims):
    (lh, ll), (rh, rl) = left, right
    dot = functools.partial(lax.dot_general, dimension_numbers=dims, preferred_element_type=jnp.float32)
    return dot(lh, rh) + (dot(lh, rl) + dot(ll, rh))


def kernel(
    n_leaf, n_probe, pieces,
    mask, block_hbm, row_hbm, col_hbm, probe_hbm, app_hbm, gram_ref,
    block, row, col, probe, probe_h, probe_l, own, swap, sib_h, sib_l,
    app, app_h, app_l, got, part, shares, total, extra, turned, kept_h, kept_l,
    load_sem, out_sem, swap_send, swap_recv, right_send, right_recv, left_send, left_recv,
    share_send, share_recv, extra_send, extra_recv,
):
    depth, rank = row.shape[0], row.shape[2]
    points, width = app.shape
    side = mask.shape[1]
    span = points // side
    half = points // 2
    piece = half // pieces
    leaf, z = lax.axis_index("leaf"), lax.axis_index("probe")
    slab = n_probe * width // n_leaf
    fan = n_leaf // n_probe
    a, b = leaf // fan, leaf % fan
    last = n_probe - 1
    ends = n_probe > 2

    loads = [
        pltpu.make_async_copy(source, target, load_sem.at[i])
        for i, (source, target) in enumerate(
            ((probe_hbm, probe), (col_hbm, col), (block_hbm, block), (row_hbm, row))
        )
    ]
    loads[0].start()
    loads[1].start()

    barrier = pltpu.get_barrier_semaphore()

    @pl.loop(1, n_leaf)
    def _(k):
        pl.semaphore_signal(
            barrier, inc=1, device_id={"leaf": (leaf + k) % n_leaf, "probe": z}, device_id_type=MESH
        )

    @pl.when(z > 0)
    def _():
        pl.semaphore_signal(barrier, inc=1, device_id={"leaf": leaf, "probe": z - 1}, device_id_type=MESH)

    @pl.when(z < last)
    def _():
        pl.semaphore_signal(barrier, inc=1, device_id={"leaf": leaf, "probe": z + 1}, device_id_type=MESH)

    @pl.when(a != z)
    def _():
        @pl.loop(0, fan)
        def _(c):
            pl.semaphore_signal(
                barrier, inc=1, device_id={"leaf": z * fan + c, "probe": a}, device_id_type=MESH
            )

    loads[0].wait()
    ph, plo = split(probe[...])
    probe_h[...] = ph
    probe_l[...] = plo
    loads[1].wait()
    loads[2].start()
    loads[3].start()
    columns = jnp.concatenate([col[level] for level in range(depth)], axis=1)
    own[...] = dot3(split(columns), (probe_h[...], probe_l[...]), CONTRACT_ROWS).reshape(own.shape)

    peers = n_leaf - 1 + jnp.where(z > 0, 1, 0) + jnp.where(z < last, 1, 0) + jnp.where(a != z, fan, 0)
    pl.semaphore_wait(barrier, peers)

    def exchange(step):
        away = 2**step
        other = leaf + (1 - 2 * ((leaf // away) % 2)) * away
        start = sum(depth - s for s in range(step))
        return start, pltpu.make_async_remote_copy(
            src_ref=own.at[pl.ds(step, depth - step)],
            dst_ref=swap.at[pl.ds(start, depth - step)],
            send_sem=swap_send.at[step],
            recv_sem=swap_recv.at[step],
            device_id={"leaf": other, "probe": z},
            device_id_type=MESH,
        )

    def near(which):
        @pl.loop(0, side // 2)
        def _(i):
            line = which * (side // 2) + i
            rows = pl.ds(pl.multiple_of(line * span, span), span)
            strips = [
                block[rows, j * span : (j + 1) * span] * mask[0, line, j].astype(jnp.float32)
                for j in range(side)
            ]
            into = pl.ds(pl.multiple_of(i * span, span), span)
            kept_h[into, :], kept_l[into, :] = split(jnp.concatenate(strips, axis=1))

        app[which * half : (which + 1) * half, :] = dot3(
            (kept_h[...], kept_l[...]), (probe_h[...], probe_l[...]), PLAIN
        )

    for step in range(depth):
        start, copy = exchange(step)
        copy.start()
        if step == 0:
            loads[2].wait()
        for which in range(2):
            if step == min(which, depth - 1):
                near(which)
        copy.wait()
        sib_h[step * rank : (step + 1) * rank, :], sib_l[step * rank : (step + 1) * rank, :] = split(
            swap[start]
        )
        for level in range(step + 1, depth):
            own[level] = own[level] + swap[start + level - step]

    def ship(source, to, slot, begin, send, recv):
        rows = pl.ds(pl.multiple_of(begin, piece), piece)
        return pltpu.make_async_remote_copy(
            src_ref=source.at[rows] if source is app else source.at[slot, rows],
            dst_ref=got.at[slot, rows],
            send_sem=send.at[slot, begin // piece],
            recv_sem=recv.at[slot, begin // piece],
            device_id={"leaf": leaf, "probe": to},
            device_id_type=MESH,
        )

    def rightward(source, slot, begin):
        return ship(source, jnp.minimum(z + 1, last), slot, begin, right_send, right_recv)

    def leftward(source, slot, begin):
        return ship(source, jnp.maximum(z - 1, 0), slot, begin, left_send, left_recv)

    loads[3].wait()
    sends_right = (z < last - 1) if ends else (z < last)
    sends_left = (z > 1) if ends else (z > 0)

    def far(which):
        rows = slice(which * half, (which + 1) * half)
        factors = jnp.concatenate([row[level, rows, :] for level in range(depth)], axis=1)
        value = app[rows, :] + dot3(split(factors), (sib_h[...], sib_l[...]), PLAIN)
        app[rows, :] = value
        app_h[rows, :], app_l[rows, :] = split(value)

    far(0)

    @pl.when(sends_right)
    def _():
        @pl.loop(0, pieces)
        def _(c):
            rightward(app, z, c * piece).start()

    far(1)

    @pl.when(sends_left)
    def _():
        @pl.loop(0, pieces)
        def _(c):
            leftward(app, z, half + c * piece).start()

    if ends:
        @pl.loop(0, pieces)
        def _(c):
            @pl.when(z == 0)
            def _():
                rightward(app, z, half + c * piece).start()

            @pl.when(z == last)
            def _():
                leftward(app, z, c * piece).start()

    keep = pltpu.make_async_copy(app, app_hbm, out_sem)
    keep.start()

    def gram(slot, source, begin, fresh):
        into = pl.ds(pl.multiple_of(slot * width, width), width)
        rows = pl.ds(pl.multiple_of(begin, half), half)
        here = (app_h[rows, :], app_l[rows, :])
        there = here if source is None else split(source[slot, rows, :])
        value = dot3(there, here, CONTRACT_ROWS)
        part[into, :] = value if fresh else part[into, :] + value

    def share(k):
        to = (leaf + k) % n_leaf
        return pltpu.make_async_remote_copy(
            src_ref=part.at[pl.ds(pl.multiple_of(to * slab, slab), slab)],
            dst_ref=shares.at[k],
            send_sem=share_send.at[k],
            recv_sem=share_recv.at[k],
            device_id={"leaf": to, "probe": z},
            device_id_type=MESH,
        )

    def give(slot):
        @pl.loop(0, fan)
        def _(c):
            to = slot * fan + c

            @pl.when(to != leaf)
            def _():
                share((to - leaf + n_leaf) % n_leaf).start()

    part[...] = jnp.zeros_like(part)

    @pl.loop(0, 2)
    def _(h):
        gram(z, None, h * half, False)

    give(z)

    @pl.loop(1, n_probe)
    def _(d):
        from_left = (z - d >= 0) & ((z < last) | (d > 1) | (not ends))
        from_right = (z + d <= last) & ((z > 0) | (d > 1) | (not ends))
        low_slot, high_slot = jnp.maximum(z - d, 0), jnp.minimum(z + d, last)

        @pl.loop(0, pieces)
        def _(c):
            up, low = c * piece, half + c * piece

            @pl.when(from_left)
            def _():
                rightward(got, low_slot, up).wait_recv()

                @pl.when(z < last)
                def _():
                    rightward(got, low_slot, up).start()

            @pl.when(from_right)
            def _():
                leftward(got, high_slot, low).wait_recv()

                @pl.when(z > 0)
                def _():
                    leftward(got, high_slot, low).start()

        @pl.loop(0, 2)
        def _(h):
            @pl.when(jnp.where(h == 0, from_left, from_right))
            def _():
                slot = jnp.where(h == 0, low_slot, high_slot)
                gram(slot, got, h * half, False)
                whole = (d > 1) | jnp.where(h == 0, z != 1, z != last - 1) | (not ends)

                @pl.when(whole)
                def _():
                    give(slot)

    if ends:
        at_low, at_high = z == 1, z == last - 1

        @pl.loop(0, pieces)
        def _(c):
            @pl.when(at_low)
            def _():
                rightward(got, z - 1, half + c * piece).wait_recv()

            @pl.when(at_high)
            def _():
                leftward(got, z + 1, c * piece).wait_recv()

        @pl.loop(0, 2)
        def _(h):
            @pl.when(jnp.where(h == 0, at_high, at_low))
            def _():
                slot = jnp.where(h == 0, jnp.minimum(z + 1, last), jnp.maximum(z - 1, 0))
                gram(slot, got, h * half, False)
                give(slot)

    total[...] = part[pl.ds(pl.multiple_of(leaf * slab, slab), slab), :]

    def holds(slot):
        return (not ends) | (((z > 0) | (slot != 1)) & ((z < last) | (slot != last - 1)))

    @pl.when(holds(a))
    def _():
        @pl.loop(1, n_leaf)
        def _(k):
            share(k).wait_recv()
            total[...] = total[...] + shares[k]

    scale = 1.0 / (points * n_leaf)

    tile = extra.shape[1]

    def trade(c, at):
        return pltpu.make_async_remote_copy(
            src_ref=total if tile == width else total.at[:, pl.ds(pl.multiple_of(c * tile, tile), tile)],
            dst_ref=extra.at[pl.ds(pl.multiple_of(at * slab, slab), slab)],
            send_sem=extra_send.at[c],
            recv_sem=extra_recv.at[at],
            device_id={"leaf": z * fan + c, "probe": a},
            device_id_type=MESH,
        )

    @pl.when(a != z)
    def _():
        @pl.loop(0, fan)
        def _(c):
            trade(c, b).start()

        @pl.loop(0, fan)
        def _(c):
            trade(c, c).wait_recv()

        turned[...] = extra[...].T
        skip = 0 if tile == slab else pl.multiple_of(b * slab, slab)
        gram_ref[...] = (total[...] + turned[pl.ds(skip, slab), :]) * scale

        @pl.loop(0, fan)
        def _(c):
            trade(c, b).wait_send()

    @pl.when(a == z)
    def _():
        gram_ref[...] = total[...] * scale

    @pl.loop(0, pieces)
    def _(c):
        up, low = c * piece, half + c * piece

        @pl.when(sends_right)
        def _():
            rightward(app, z, up).wait_send()

        @pl.when(sends_left)
        def _():
            leftward(app, z, low).wait_send()

        if ends:

            @pl.when(z == 0)
            def _():
                rightward(app, z, low).wait_send()

            @pl.when(z == last)
            def _():
                leftward(app, z, up).wait_send()

        @pl.loop(1, n_probe)
        def _(d):
            @pl.when((z - d >= 0) & (z < last))
            def _():
                rightward(got, jnp.maximum(z - d, 0), up).wait_send()

            @pl.when((z + d <= last) & (z > 0))
            def _():
                leftward(got, jnp.minimum(z + d, last), low).wait_send()

    @pl.loop(1, n_leaf)
    def _(k):
        @pl.when(holds(((leaf + k) % n_leaf) // fan))
        def _():
            share(k).wait_send()

    keep.wait()


def local(n_leaf, n_probe, leaf_blocks, block_mask, row_factor_stack, column_factor_stack, probes):
    depth, points, rank = row_factor_stack.shape
    width = probes.shape[1]
    slab = n_probe * width // n_leaf
    fan = n_leaf // n_probe
    pieces = 4
    tile = slab if slab % 128 == 0 else width
    f32, bf16 = jnp.float32, jnp.bfloat16
    dma = pltpu.SemaphoreType.DMA
    hbm = pl.BlockSpec(memory_space=pltpu.HBM)
    return pl.pallas_call(
        functools.partial(kernel, n_leaf, n_probe, pieces),
        out_shape=(
            jax.ShapeDtypeStruct((points, width), f32),
            jax.ShapeDtypeStruct((slab, width), f32),
        ),
        in_specs=[pl.BlockSpec(memory_space=pltpu.SMEM), hbm, hbm, hbm, hbm],
        out_specs=(hbm, pl.BlockSpec(memory_space=pltpu.VMEM)),
        scratch_shapes=[
            pltpu.VMEM((points, points), f32),
            pltpu.VMEM((depth, points, rank), f32),
            pltpu.VMEM((depth, points, rank), f32),
            pltpu.VMEM((points, width), f32),
            pltpu.VMEM((points, width), bf16),
            pltpu.VMEM((points, width), bf16),
            pltpu.VMEM((depth, rank, width), f32),
            pltpu.VMEM((depth * (depth + 1) // 2, rank, width), f32),
            pltpu.VMEM((depth * rank, width), bf16),
            pltpu.VMEM((depth * rank, width), bf16),
            pltpu.VMEM((points, width), f32),
            pltpu.VMEM((points, width), bf16),
            pltpu.VMEM((points, width), bf16),
            pltpu.VMEM((n_probe, points, width), f32),
            pltpu.VMEM((n_probe * width, width), f32),
            pltpu.VMEM((n_leaf, slab, width), f32),
            pltpu.VMEM((slab, width), f32),
            pltpu.VMEM((width, tile), f32),
            pltpu.VMEM((tile, width), f32),
            pltpu.VMEM((points // 2, points), bf16),
            pltpu.VMEM((points // 2, points), bf16),
            dma((4,)),
            dma,
            dma((depth,)),
            dma((depth,)),
            dma((n_probe, 2 * pieces)),
            dma((n_probe, 2 * pieces)),
            dma((n_probe, 2 * pieces)),
            dma((n_probe, 2 * pieces)),
            dma((n_leaf,)),
            dma((n_leaf,)),
            dma((fan,)),
            dma((fan,)),
        ],
        compiler_params=pltpu.CompilerParams(
            collective_id=0, has_side_effects=True, vmem_limit_bytes=67043328
        ),
    )(block_mask, leaf_blocks, row_factor_stack, column_factor_stack, probes)


def solution(mesh):
    return jax.shard_map(
        functools.partial(local, mesh.shape["leaf"], mesh.shape["probe"]),
        mesh=mesh,
        in_specs=(
            P("leaf", None),
            P("leaf", None, None),
            P(None, "leaf", None),
            P(None, "leaf", None),
            P("leaf", "probe"),
        ),
        out_specs=(P("leaf", "probe"), P("leaf", "probe")),
        check_vma=False,
    )
```
